512 devices in a mesh: dp: 16 (over x_lo, y, core), vocab: 32 (over z, x_hi).
Axes of the slice: x: 4 (x_hi: 2, x_lo: 2; x = x_hi * 2 + x_lo), y: 4, z: 16, core: 2. Of those that a mesh axis runs over, the one named last changes fastest.
Arguments:
- passage_hidden: bfloat16 [2048, 2048], P('dp'), may hold values from -7 to 7
- passage_lengths: int32 [32], P('dp'), may hold values from 16 to 64, as said below
- query_ids: int32 [32, 16], P('dp'), may hold values from 0 to 131071
- query_lengths: int32 [32], P('dp'), may hold values from 4 to 16, as said below
- positives: int32 [32], replicated, may hold values from 0 to 31, each once
- head: bfloat16 [2048, 131072], P('dp', 'vocab'), may hold values from -0.125 to 0.125
- df_prev: float32 [131072], P('vocab'), may hold values from 1 to 4096
Outputs:
- head_grad: float32 [2048, 131072], P('dp', 'vocab')
- scores: float32 [32, 32], replicated
The draws below stay inside these ranges and needn't reach their ends.
Inputs may be any that keep to these rules, and one draw needn't show every extreme that they name: `passage_lengths`: some passage fills all 64 slots. `query_lengths`: some query fills all 16 slots. `positives`: each passage is the positive of exactly one query.
All inputs are finite; a program needn't handle non-finite values.
Results may differ from the reference program's by a relative error of at most 0.00064.
Values may be sent and summed in bfloat16 or wider, within the bound.
No kernel may reach another device: no remote copies, remote signals or barrier semaphores. Data moves between devices by JAX's collectives and lax.ppermute only.
A program may use at most 64 MiB of HBM per device.

```python
import math
import jax
import jax.numpy as jnp
import numpy as np
from jax import lax

D = 2048
V_DEV = 4096
PLEN = 64
QLEN = 16
V = 131072
PASSAGES = 32
QUERIES = 32


def draw_passage_hidden(key, part):
    first_key, second_key = jax.random.split(key)
    common = jnp.clip(jax.random.normal(first_key, (PASSAGES, 1, D), jnp.float32), -5.0, 5.0)
    jitter = jnp.clip(jax.random.normal(second_key, (PASSAGES, PLEN, D), jnp.float32), -5.0, 5.0)
    mixed = 0.8 * common + 0.6 * jitter
    return mixed.reshape(PASSAGES * PLEN, D).astype(jnp.bfloat16)


def draw_sizes(key, count, longest):
    first_key, second_key = jax.random.split(key)
    values = jax.random.randint(first_key, (count,), longest // 4, longest + 1, dtype=jnp.int32)
    chosen = jax.random.randint(second_key, (), 0, count, dtype=jnp.int32)
    return jnp.where(jnp.arange(count, dtype=jnp.int32) == chosen, longest, values).astype(jnp.int32)


def draw_passage_lengths(key, part):
    return draw_sizes(jax.random.fold_in(key, 11), PASSAGES, PLEN)


def draw_query_lengths(key, part):
    return draw_sizes(jax.random.fold_in(key, 23), QUERIES, QLEN)


def touch_ends(array, rng, low, top_value):
    shape = array.shape
    spot = [jax.random.randint(jax.random.fold_in(rng, axis), (), 0, shape[axis]) for axis in range(len(shape))]
    array = array.at[tuple(spot)].set(low)
    longest = shape.index(max(shape))
    spot[longest] = (spot[longest] + 1) % shape[longest]
    return array.at[tuple(spot)].set(top_value)


def shard_levels(key, shape, pieces, smallest, top_value):
    loudness, own = 1.0, jax.random.fold_in(key, 6)
    for position, parts in pieces:
        steps = jnp.exp(jax.random.uniform(jax.random.fold_in(own, position), (parts,), jnp.float32, smallest / len(pieces), top_value / len(pieces)))
        loudness = loudness * jnp.repeat(steps, shape[position] // parts).reshape([-1 if axis == position else 1 for axis in range(len(shape))])
    return loudness


def ranked_wide(key, extent, amount, lean):
    portions = [min(1 << octave, amount + 1 - (1 << octave)) * (1 << 20) // math.isqrt((1 << octave) ** lean) + 1 for octave in range((amount + 1).bit_length()) if 1 << octave <= amount]
    spread = 1 + sum(portions) // (1 << 30)
    listing = np.cumsum(np.array([max(1, weight // spread) for weight in portions]))
    ticket = jax.random.randint(jax.random.fold_in(key, 1), extent, 0, int(listing[len(portions) - 1]))
    start = jnp.left_shift(1, jnp.searchsorted(jnp.asarray(listing, jnp.int32), ticket, side="right").astype(jnp.int32))
    standing = start - 1 + jax.random.randint(jax.random.fold_in(key, 4), extent, 0, 1 << 30) % jnp.minimum(start, amount + 1 - start)
    return jax.random.permutation(jax.random.fold_in(key, 2), amount)[standing].astype(jnp.int32)


def noise(own_key, dims, spread, bound, pieces=(), held_as=jnp.bfloat16):
    values = jax.random.normal(own_key, dims, jnp.float32) * spread
    if len(pieces) > 0:
        values = shard_levels(own_key, dims, pieces, -0.22, 0.18) * values
    return jnp.clip(values, min=-bound, max=bound).astype(held_as)


def setup_inputs(seed: int = 0) -> dict:
    streams_of = jax.random.split(jax.random.key(seed), 8)
    return {
        "passage_hidden": draw_passage_hidden(jax.random.fold_in(streams_of[7], 71), 0),
        "passage_lengths": draw_passage_lengths(jax.random.fold_in(streams_of[7], 71), 0),
        "query_ids": touch_ends(ranked_wide(streams_of[2], (QUERIES, QLEN), V, 2), jax.random.fold_in(streams_of[2], 3), 0, V - 1).astype(jnp.int32),
        "query_lengths": draw_query_lengths(jax.random.fold_in(streams_of[7], 71), 0),
        "positives": jax.random.permutation(streams_of[4], PASSAGES).astype(jnp.int32),
        "head": noise(streams_of[5], (D, V), D ** -0.5, 0.125, ((0, 16), (1, 32))),
        "df_prev": jnp.clip(jnp.exp(math.log(4096.0) - 8.317766 * jax.random.uniform(streams_of[6], (V,), jnp.float32) ** shard_levels(streams_of[6], (V,), ((0, 32),), -0.2, 0.2)), 1.0, 4096.0),
    }


flops_weight = 0.3

def ranking_grad(scores, chosen, query_total):
    columns = scores.shape[1]
    onehot = (jnp.arange(columns, dtype=jnp.int32)[None, :] == chosen[:, None]).astype(jnp.float32)
    own_score = lax.optimization_barrier(jnp.sum(scores * onehot, axis=1, keepdims=True))
    sigmas = jax.nn.sigmoid(scores - own_score)
    return (sigmas - onehot * lax.optimization_barrier(jnp.sum(sigmas, axis=1, keepdims=True))) / query_total

def reference(passage_hidden, passage_lengths, query_ids, query_lengths, positives, head, df_prev):
    passage_count = passage_lengths.shape[0]
    query_count = query_ids.shape[0]
    block_width = V_DEV
    block_count = head.shape[1] // block_width
    positions = jnp.arange(PLEN, dtype=jnp.int32)
    token_mask = (positions[None, :] < passage_lengths[:, None]).astype(jnp.float32)
    token_weight = token_mask / passage_lengths.astype(jnp.float32)[:, None]

    def pool_block(index):
        columns = lax.dynamic_slice_in_dim(head, index * block_width, block_width, 1)
        logits = jnp.dot(passage_hidden, columns, preferred_element_type=jnp.float32)
        activation = jnp.log1p(jax.nn.softplus(logits))
        return lax.optimization_barrier(jnp.sum(activation.reshape(passage_count, PLEN, block_width) * token_weight[:, :, None], axis=1))
    rep_blocks = lax.map(pool_block, jnp.arange(block_count, dtype=jnp.int32))
    passage_rep = rep_blocks.transpose(1, 0, 2).reshape(passage_count, block_count * block_width)
    doc_freq = df_prev + lax.optimization_barrier(jnp.sum(1.0 - jnp.exp(-2.0 * passage_rep), axis=0))
    term_weight = jnp.log1p(doc_freq)
    query_mask = (jnp.arange(QLEN, dtype=jnp.int32)[None, :] < query_lengths[:, None]).astype(jnp.float32)
    row_index = jnp.broadcast_to(jnp.arange(query_count, dtype=jnp.int32)[:, None], query_ids.shape)
    query_bag = jnp.zeros((query_count, head.shape[1]), jnp.float32).at[row_index, query_ids].add(query_mask)
    scores = jnp.dot(query_bag, passage_rep.T, precision=lax.Precision.HIGHEST, preferred_element_type=jnp.float32)
    score_grad = ranking_grad(scores, positives, query_count)
    rep_grad = jnp.dot(score_grad.T, query_bag, precision=lax.Precision.HIGHEST, preferred_element_type=jnp.float32)
    rep_grad = rep_grad + 2.0 * flops_weight / passage_count * term_weight * lax.optimization_barrier(jnp.mean(passage_rep, axis=0))

    def grad_block(index):
        columns = lax.dynamic_slice_in_dim(head, index * block_width, block_width, 1)
        logits = jnp.dot(passage_hidden, columns, preferred_element_type=jnp.float32)
        softened = jax.nn.softplus(logits)
        slope_term = jax.nn.sigmoid(logits) / (1.0 + softened)
        rep_slice = lax.dynamic_slice_in_dim(rep_grad, index * block_width, block_width, 1)
        logit_grad = ((token_weight[:, :, None] * rep_slice[:, None, :]).reshape(logits.shape) * slope_term).astype(jnp.bfloat16)
        return lax.dot_general(passage_hidden, logit_grad, (((0,), (0,)), ((), ())), preferred_element_type=jnp.float32)
    grad_blocks = lax.map(grad_block, jnp.arange(block_count, dtype=jnp.int32))
    head_grad = grad_blocks.transpose(1, 0, 2).reshape(head.shape[0], block_count * block_width)
    return (head_grad, scores)
```

```python
import jax
import jax.numpy as jnp
from jax import lax
from jax.sharding import Mesh, PartitionSpec as P

flops_weight = 0.3
DP = ("xl", "y", "c")
VOCAB = ("z", "xh")
PLANE = ("xl", "y", "c", "xh")


def ranking_grad(scores, chosen, query_total):
    columns = scores.shape[1]
    onehot = (jnp.arange(columns, dtype=jnp.int32)[None, :] == chosen[:, None]).astype(jnp.float32)
    own_score = jnp.sum(scores * onehot, axis=1, keepdims=True)
    sigmas = jax.nn.sigmoid(scores - own_score)
    return (sigmas - onehot * jnp.sum(sigmas, axis=1, keepdims=True)) / query_total


def spread(value, axes):
    count = lax.axis_size(axes)
    return lax.all_to_all(
        jnp.broadcast_to(value[None], (count,) + value.shape), axes, 0, 0, tiled=True
    )


def local(passage_hidden, passage_lengths, query_ids, query_lengths, positives, head, df_prev):
    dp_count = lax.axis_size(DP)
    dp_index = lax.axis_index(DP)
    vocab_index = lax.axis_index(VOCAB)
    width_local = head.shape[1]
    column_count = width_local // dp_count
    query_slots = query_ids.shape[1]
    packed = jnp.concatenate([query_ids, query_lengths[:, None], passage_lengths[:, None]], axis=1)
    packed = spread(packed, DP).reshape(-1, query_slots + 2)
    query_tokens = packed[:, :query_slots]
    query_sizes = packed[:, query_slots]
    passage_sizes = packed[:, query_slots + 1]
    head_block = lax.all_to_all(head, DP, split_axis=1, concat_axis=0, tiled=True)
    hidden_all = lax.all_gather(passage_hidden, DP, axis=0, tiled=True)
    passage_count = passage_sizes.shape[0]
    seq_span = hidden_all.shape[0] // passage_count
    logits = jnp.dot(hidden_all, head_block, preferred_element_type=jnp.float32)
    softened = jax.nn.softplus(logits)
    activation = jnp.log1p(softened)
    slope_term = jax.nn.sigmoid(logits) / (1.0 + softened)
    positions = jnp.arange(seq_span, dtype=jnp.int32)
    token_mask = (positions[None, :] < passage_sizes[:, None]).astype(jnp.float32)
    token_weight = token_mask / passage_sizes.astype(jnp.float32)[:, None]
    passage_rep = jnp.sum(
        activation.reshape(passage_count, seq_span, column_count) * token_weight[:, :, None], axis=1
    )
    first_column = dp_index * column_count
    doc_freq = lax.dynamic_slice_in_dim(df_prev, first_column, column_count, 0) + jnp.sum(
        1.0 - jnp.exp(-2.0 * passage_rep), axis=0
    )
    term_weight = jnp.log1p(doc_freq)
    column_ids = (
        vocab_index * width_local + first_column + jnp.arange(column_count, dtype=jnp.int32)
    )
    query_mask = jnp.arange(query_slots, dtype=jnp.int32)[None, :] < query_sizes[:, None]
    matches = (query_tokens[:, :, None] == column_ids[None, None, :]) & query_mask[:, :, None]
    query_bag = jnp.sum(matches.astype(jnp.float32), axis=1)
    partial_scores = jnp.dot(
        query_bag,
        passage_rep.T,
        precision=lax.Precision.HIGHEST,
        preferred_element_type=jnp.float32,
    )
    query_total = positives.shape[0]
    plane_scores = jnp.sum(spread(partial_scores, PLANE), axis=0)
    scores = jnp.sum(spread(plane_scores, "z"), axis=0)
    score_grad = ranking_grad(scores, positives, query_total)
    rep_grad = jnp.dot(
        score_grad.T, query_bag, precision=lax.Precision.HIGHEST, preferred_element_type=jnp.float32
    )
    rep_grad = rep_grad + 2.0 * flops_weight / passage_count * term_weight * jnp.mean(
        passage_rep, axis=0
    )
    logit_grad = (
        (token_weight[:, :, None] * rep_grad[:, None, :]).reshape(logits.shape) * slope_term
    ).astype(jnp.bfloat16)
    grad_block = lax.dot_general(
        hidden_all, logit_grad, (((0,), (0,)), ((), ())), preferred_element_type=jnp.float32
    )
    head_grad = lax.all_to_all(grad_block, DP, split_axis=0, concat_axis=1, tiled=True)
    return (head_grad, scores)


def solution(mesh):
    fine = Mesh(mesh.devices.reshape(2, 4, 2, 16, 2), DP + VOCAB)
    return jax.shard_map(
        local,
        mesh=fine,
        in_specs=(
            P(DP, None),
            P(DP),
            P(DP, None),
            P(DP),
            P(),
            P(DP, VOCAB),
            P(VOCAB),
        ),
        out_specs=(P(DP, VOCAB), P()),
        check_vma=False,
    )
```

```python
import jax
import jax.numpy as jnp
from jax import lax
from jax.sharding import Mesh, PartitionSpec as P


flops_weight = 0.3
DP = ("xl", "y", "c")
VOCAB = ("z", "xh")
PLANE = ("xl", "y", "c", "xh")
X = ("xl", "xh")


def ranking_grad(scores, chosen, query_total):
    columns = scores.shape[1]
    onehot = (jnp.arange(columns, dtype=jnp.int32)[None, :] == chosen[:, None]).astype(jnp.float32)
    own_score = jnp.sum(scores * onehot, axis=1, keepdims=True)
    sigmas = jax.nn.sigmoid(scores - own_score)
    return (sigmas - onehot * jnp.sum(sigmas, axis=1, keepdims=True)) / query_total


def spread(value, axes):
    count = lax.axis_size(axes)
    return lax.all_to_all(
        jnp.broadcast_to(value[None], (count,) + value.shape), axes, 0, 0, tiled=True
    )


def send_up(value, axis):
    count = lax.axis_size(axis)
    return lax.ppermute(value, axis, [(i, (i + 1) % count) for i in range(count)])


def send_down(value, axis):
    count = lax.axis_size(axis)
    return lax.ppermute(value, axis, [((i + 1) % count, i) for i in range(count)])


def x_slot(position):
    return (position % 2) * 2 + position // 2


def send_x_up(value):
    return lax.ppermute(value, X, [(x_slot(i), x_slot((i + 1) % 4)) for i in range(4)])


def send_x_down(value):
    return lax.ppermute(value, X, [(x_slot((i + 1) % 4), x_slot(i)) for i in range(4)])


def swap_x(value):
    return lax.ppermute(value, X, [(x_slot(i), x_slot(i ^ 3)) for i in range(4)])


def swap_cores(value):
    return lax.ppermute(value, "c", [(0, 1), (1, 0)])


STEPS = ((0, 0), (0, 3), (0, 1), (1, 0), (0, 2), (1, 3), (1, 1), (1, 2))


def gather_hidden(own):
    rows = own.shape[0] // 2
    below = send_up(own, "y")
    above = send_down(own, "y")
    side = swap_x(own)
    near = jnp.concatenate([own, below, above, side])
    far_low = send_up(below[:rows], "y")
    far_high = send_down(above[rows:], "y")
    side_below = send_x_up(below)
    side_above = send_x_down(above)
    near_other = swap_cores(near)
    corner_low = send_x_up(far_low)
    corner_high = send_x_down(far_high)
    rest = jnp.concatenate([far_low, far_high, side_below, side_above, corner_low, corner_high])
    rest_other = swap_cores(rest)
    return jnp.concatenate([near, rest, near_other, rest_other])


def gathered_passages():
    spot = jnp.arange(32, dtype=jnp.int32)
    piece, half, other = spot // 2 % 8, spot % 2, spot // 16
    flip = sum(jnp.where(piece == k, f, 0) for k, (f, _) in enumerate(STEPS))
    step = sum(jnp.where(piece == k, s, 0) for k, (_, s) in enumerate(STEPS))
    xl, y, c = lax.axis_index("xl"), lax.axis_index("y"), lax.axis_index("c")
    return ((((xl + flip) & 1) * 4 + ((y + step) & 3)) * 2 + (c ^ other)) * 2 + half


def local(passage_hidden, passage_lengths, query_ids, query_lengths, positives, head, df_prev):
    dp_count = lax.axis_size(DP)
    dp_index = lax.axis_index(DP)
    vocab_index = lax.axis_index(VOCAB)
    width_local = head.shape[1]
    column_count = width_local // dp_count
    query_slots = query_ids.shape[1]
    packed = jnp.concatenate([query_ids, query_lengths[:, None], passage_lengths[:, None]], axis=1)
    packed = spread(packed, DP).reshape(-1, query_slots + 2)
    query_tokens = packed[:, :query_slots]
    query_sizes = packed[:, query_slots]
    hidden_all = gather_hidden(passage_hidden)
    passages = gathered_passages()
    passage_count = packed.shape[0]
    placed = passages[:, None] == jnp.arange(passage_count, dtype=jnp.int32)[None, :]
    passage_sizes = jnp.sum(jnp.where(placed, packed[:, query_slots + 1][None, :], 0), axis=1)
    placed = placed.astype(jnp.float32)
    head_block = lax.all_to_all(head, DP, split_axis=1, concat_axis=0, tiled=True)
    seq_span = hidden_all.shape[0] // passage_count
    logits = jnp.dot(hidden_all, head_block, preferred_element_type=jnp.float32)
    softened = jax.nn.softplus(logits)
    activation = jnp.log1p(softened)
    slope_term = jax.nn.sigmoid(logits) / (1.0 + softened)
    positions = jnp.arange(seq_span, dtype=jnp.int32)
    token_mask = (positions[None, :] < passage_sizes[:, None]).astype(jnp.float32)
    token_weight = token_mask / passage_sizes.astype(jnp.float32)[:, None]
    passage_rep = jnp.sum(
        activation.reshape(passage_count, seq_span, column_count) * token_weight[:, :, None], axis=1
    )
    first_column = dp_index * column_count
    doc_freq = lax.dynamic_slice_in_dim(df_prev, first_column, column_count, 0) + jnp.sum(
        1.0 - jnp.exp(-2.0 * passage_rep), axis=0
    )
    term_weight = jnp.log1p(doc_freq)
    column_ids = (
        vocab_index * width_local + first_column + jnp.arange(column_count, dtype=jnp.int32)
    )
    query_mask = jnp.arange(query_slots, dtype=jnp.int32)[None, :] < query_sizes[:, None]
    matches = (query_tokens[:, :, None] == column_ids[None, None, :]) & query_mask[:, :, None]
    query_bag = jnp.sum(matches.astype(jnp.float32), axis=1)
    partial_scores = jnp.dot(
        query_bag,
        passage_rep.T,
        precision=lax.Precision.HIGHEST,
        preferred_element_type=jnp.float32,
    )
    partial_scores = jnp.dot(partial_scores, placed, precision=lax.Precision.HIGHEST)
    query_total = positives.shape[0]
    plane_scores = jnp.sum(spread(partial_scores, PLANE), axis=0)
    scores = jnp.sum(spread(plane_scores, "z"), axis=0)
    score_grad = ranking_grad(scores, positives, query_total)
    score_grad = jnp.dot(placed, score_grad.T, precision=lax.Precision.HIGHEST)
    rep_grad = jnp.dot(
        score_grad, query_bag, precision=lax.Precision.HIGHEST, preferred_element_type=jnp.float32
    )
    rep_grad = rep_grad + 2.0 * flops_weight / passage_count * term_weight * jnp.mean(
        passage_rep, axis=0
    )
    logit_grad = (
        (token_weight[:, :, None] * rep_grad[:, None, :]).reshape(logits.shape) * slope_term
    ).astype(jnp.bfloat16)
    grad_block = lax.dot_general(
        hidden_all, logit_grad, (((0,), (0,)), ((), ())), preferred_element_type=jnp.float32
    )
    head_grad = lax.all_to_all(grad_block, DP, split_axis=0, concat_axis=1, tiled=True)
    return (head_grad, scores)


def solution(mesh):
    fine = Mesh(mesh.devices.reshape(2, 4, 2, 16, 2), DP + VOCAB)
    return jax.shard_map(
        local,
        mesh=fine,
        in_specs=(
            P(DP, None),
            P(DP),
            P(DP, None),
            P(DP),
            P(),
            P(DP, VOCAB),
            P(VOCAB),
        ),
        out_specs=(P(DP, VOCAB), P()),
        check_vma=False,
    )
```

```python
import jax
import jax.numpy as jnp
from jax import lax
from jax.experimental import pallas as pl
from jax.sharding import Mesh, PartitionSpec as P


flops_weight = 0.3
DP = ("xl", "y", "c")
VOCAB = ("z", "xh")
PLANE = ("xl", "y", "c", "xh")
X = ("xl", "xh")


def ranking_grad(scores, chosen, query_total):
    columns = scores.shape[1]
    onehot = (jnp.arange(columns, dtype=jnp.int32)[None, :] == chosen[:, None]).astype(jnp.float32)
    own_score = jnp.sum(scores * onehot, axis=1, keepdims=True)
    sigmas = jax.nn.sigmoid(scores - own_score)
    return (sigmas - onehot * jnp.sum(sigmas, axis=1, keepdims=True)) / query_total


def spread(value, axes):
    count = lax.axis_size(axes)
    return lax.all_to_all(
        jnp.broadcast_to(value[None], (count,) + value.shape), axes, 0, 0, tiled=True
    )


def send_up(value, axis):
    count = lax.axis_size(axis)
    return lax.ppermute(value, axis, [(i, (i + 1) % count) for i in range(count)])


def send_down(value, axis):
    count = lax.axis_size(axis)
    return lax.ppermute(value, axis, [((i + 1) % count, i) for i in range(count)])


def x_slot(position):
    return (position % 2) * 2 + position // 2


def send_x_up(value):
    return lax.ppermute(value, X, [(x_slot(i), x_slot((i + 1) % 4)) for i in range(4)])


def send_x_down(value):
    return lax.ppermute(value, X, [(x_slot((i + 1) % 4), x_slot(i)) for i in range(4)])


def swap_x(value):
    return lax.ppermute(value, X, [(x_slot(i), x_slot(i ^ 3)) for i in range(4)])


def swap_cores(value):
    return lax.ppermute(value, "c", [(0, 1), (1, 0)])


STEPS = ((0, 0), (0, 3), (0, 1), (1, 0), (0, 2), (1, 3), (1, 1), (1, 2))


def gather_hidden(own):
    rows = own.shape[0] // 2
    below = send_up(own, "y")
    above = send_down(own, "y")
    side = swap_x(own)
    near = jnp.concatenate([own, below, above, side])
    far_low = send_up(below[:rows], "y")
    far_high = send_down(above[rows:], "y")
    side_below = send_x_up(below)
    side_above = send_x_down(above)
    near_other = swap_cores(near)
    corner_low = send_x_up(far_low)
    corner_high = send_x_down(far_high)
    rest = jnp.concatenate([far_low, far_high, side_below, side_above, corner_low, corner_high])
    rest_other = swap_cores(rest)
    return near, near_other, rest, rest_other


def gathered_passages():
    spot = jnp.arange(32, dtype=jnp.int32)
    piece, half, other = spot // 16 * 4 + spot // 2 % 4, spot % 2, spot // 8 % 2
    flip = sum(jnp.where(piece == k, f, 0) for k, (f, _) in enumerate(STEPS))
    step = sum(jnp.where(piece == k, s, 0) for k, (_, s) in enumerate(STEPS))
    xl, y, c = lax.axis_index("xl"), lax.axis_index("y"), lax.axis_index("c")
    return ((((xl + flip) & 1) * 4 + ((y + step) & 3)) * 2 + (c ^ other)) * 2 + half


UNPACK = 4


def unpack_rows(packet_ref, out_ref):
    _, rows, columns = packet_ref.shape
    for k in range(UNPACK):
        packet = packet_ref[k]
        unscale = jnp.exp2(-packet[rows - 8 : rows - 7])
        out_ref[:, k * columns : (k + 1) * columns] = packet[: rows - 8] * unscale


def return_rows(grad_block, dp_count):
    depth, columns = grad_block.shape
    peak = jnp.max(jnp.abs(grad_block))
    power = jnp.clip(jnp.floor(14.0 - jnp.log2(peak)), -120.0, 120.0)
    scaled = (grad_block * jnp.exp2(power)).reshape(dp_count, depth // dp_count, columns)
    tag = jnp.full((dp_count, 8, columns), power)
    packet = jnp.concatenate([scaled, tag], axis=1).astype(jnp.float16)
    packet = lax.all_to_all(packet, DP, 0, 0, tiled=True).astype(jnp.float32)
    rows = depth // dp_count
    return pl.pallas_call(
        unpack_rows,
        grid=(dp_count // UNPACK,),
        in_specs=[pl.BlockSpec((UNPACK, rows + 8, columns), lambda i: (i, 0, 0))],
        out_specs=pl.BlockSpec((rows, UNPACK * columns), lambda i: (0, i)),
        out_shape=jax.ShapeDtypeStruct((rows, dp_count * columns), jnp.float32),
        name="unpack_rows",
    )(packet)


def local(passage_hidden, passage_lengths, query_ids, query_lengths, positives, head, df_prev):
    dp_count = lax.axis_size(DP)
    dp_index = lax.axis_index(DP)
    vocab_index = lax.axis_index(VOCAB)
    width_local = head.shape[1]
    column_count = width_local // dp_count
    query_slots = query_ids.shape[1]
    packed = jnp.concatenate([query_ids, query_lengths[:, None], passage_lengths[:, None]], axis=1)
    packed = spread(packed, DP).reshape(-1, query_slots + 2)
    query_tokens = packed[:, :query_slots]
    query_sizes = packed[:, query_slots]
    groups = gather_hidden(passage_hidden)
    passages = gathered_passages()
    passage_count = packed.shape[0]
    placed = passages[:, None] == jnp.arange(passage_count, dtype=jnp.int32)[None, :]
    passage_sizes = jnp.sum(jnp.where(placed, packed[:, query_slots + 1][None, :], 0), axis=1)
    placed = placed.astype(jnp.float32)
    head_block = lax.all_to_all(head, DP, split_axis=1, concat_axis=0, tiled=True)
    group_rows = groups[0].shape[0]
    seq_span = group_rows * len(groups) // passage_count
    logits = [jnp.dot(rows, head_block, preferred_element_type=jnp.float32) for rows in groups]
    softened = [jax.nn.softplus(part) for part in logits]
    slope_term = [jax.nn.sigmoid(part) / (1.0 + soft) for part, soft in zip(logits, softened)]
    positions = jnp.arange(seq_span, dtype=jnp.int32)
    token_mask = (positions[None, :] < passage_sizes[:, None]).astype(jnp.float32)
    token_weight = token_mask / passage_sizes.astype(jnp.float32)[:, None]
    weight_of = jnp.split(token_weight, len(groups))
    passage_rep = jnp.concatenate(
        [
            jnp.sum(jnp.log1p(soft).reshape(-1, seq_span, column_count) * weight[:, :, None], axis=1)
            for soft, weight in zip(softened, weight_of)
        ]
    )
    first_column = dp_index * column_count
    doc_freq = lax.dynamic_slice_in_dim(df_prev, first_column, column_count, 0) + jnp.sum(
        1.0 - jnp.exp(-2.0 * passage_rep), axis=0
    )
    term_weight = jnp.log1p(doc_freq)
    column_ids = (
        vocab_index * width_local + first_column + jnp.arange(column_count, dtype=jnp.int32)
    )
    query_mask = jnp.arange(query_slots, dtype=jnp.int32)[None, :] < query_sizes[:, None]
    matches = (query_tokens[:, :, None] == column_ids[None, None, :]) & query_mask[:, :, None]
    query_bag = jnp.sum(matches.astype(jnp.float32), axis=1)
    partial_scores = jnp.dot(
        query_bag,
        passage_rep.T,
        precision=lax.Precision.HIGHEST,
        preferred_element_type=jnp.float32,
    )
    partial_scores = jnp.dot(partial_scores, placed, precision=lax.Precision.HIGHEST)
    query_total = positives.shape[0]
    plane_scores = jnp.sum(spread(partial_scores, PLANE), axis=0)
    scores = jnp.sum(spread(plane_scores, "z"), axis=0)
    score_grad = ranking_grad(scores, positives, query_total)
    score_grad = jnp.dot(placed, score_grad.T, precision=lax.Precision.HIGHEST)
    rep_grad = jnp.dot(
        score_grad, query_bag, precision=lax.Precision.HIGHEST, preferred_element_type=jnp.float32
    )
    rep_grad = rep_grad + 2.0 * flops_weight / passage_count * term_weight * jnp.mean(
        passage_rep, axis=0
    )
    grad_block = 0.0
    for rows, weight, rep, slope in zip(
        groups, weight_of, jnp.split(rep_grad, len(groups)), slope_term
    ):
        logit_grad = (weight[:, :, None] * rep[:, None, :]).reshape(slope.shape) * slope
        grad_block += lax.dot_general(
            rows,
            logit_grad.astype(jnp.bfloat16),
            (((0,), (0,)), ((), ())),
            preferred_element_type=jnp.float32,
        )
    return (return_rows(grad_block, dp_count), scores)


def solution(mesh):
    fine = Mesh(mesh.devices.reshape(2, 4, 2, 16, 2), DP + VOCAB)
    return jax.shard_map(
        local,
        mesh=fine,
        in_specs=(
            P(DP, None),
            P(DP),
            P(DP, None),
            P(DP),
            P(),
            P(DP, VOCAB),
            P(VOCAB),
        ),
        out_specs=(P(DP, VOCAB), P()),
        check_vma=False,
    )
```

```python
import jax
import jax.numpy as jnp
from jax import lax
from jax.experimental.layout import Layout, with_layout_constraint
from jax.sharding import Mesh, PartitionSpec as P


flops_weight = 0.3
DP = ("xl", "y", "c")
VOCAB = ("z", "xh")
PLANE = ("xl", "y", "c", "xh")
X = ("xl", "xh")


def ranking_grad(scores, chosen, query_total):
    columns = scores.shape[1]
    onehot = (jnp.arange(columns, dtype=jnp.int32)[None, :] == chosen[:, None]).astype(jnp.float32)
    own_score = jnp.sum(scores * onehot, axis=1, keepdims=True)
    sigmas = jax.nn.sigmoid(scores - own_score)
    return (sigmas - onehot * jnp.sum(sigmas, axis=1, keepdims=True)) / query_total


def spread(value, axes):
    count = lax.axis_size(axes)
    return lax.all_to_all(
        jnp.broadcast_to(value[None], (count,) + value.shape), axes, 0, 0, tiled=True
    )


def send_up(value, axis):
    count = lax.axis_size(axis)
    return lax.ppermute(value, axis, [(i, (i + 1) % count) for i in range(count)])


def send_down(value, axis):
    count = lax.axis_size(axis)
    return lax.ppermute(value, axis, [((i + 1) % count, i) for i in range(count)])


def x_slot(position):
    return (position % 2) * 2 + position // 2


def send_x_up(value):
    return lax.ppermute(value, X, [(x_slot(i), x_slot((i + 1) % 4)) for i in range(4)])


def send_x_down(value):
    return lax.ppermute(value, X, [(x_slot((i + 1) % 4), x_slot(i)) for i in range(4)])


def swap_x(value):
    return lax.ppermute(value, X, [(x_slot(i), x_slot(i ^ 3)) for i in range(4)])


def swap_cores(value):
    return lax.ppermute(value, "c", [(0, 1), (1, 0)])


STEPS = ((0, 0), (0, 3), (0, 1), (1, 0), (0, 2), (1, 3), (1, 1), (1, 2))


def gather_hidden(own):
    rows = own.shape[0] // 2
    below = send_up(own, "y")
    above = send_down(own, "y")
    side = swap_x(own)
    near = jnp.concatenate([own, below, above, side])
    far_low = send_up(below[:rows], "y")
    far_high = send_down(above[rows:], "y")
    side_below = send_x_up(below)
    side_above = send_x_down(above)
    near_other = swap_cores(near)
    corner_low = send_x_up(far_low)
    corner_high = send_x_down(far_high)
    rest = jnp.concatenate([far_low, far_high, side_below, side_above, corner_low, corner_high])
    rest_other = swap_cores(rest)
    return jnp.concatenate([near, rest, near_other, rest_other])


def gathered_passages():
    spot = jnp.arange(32, dtype=jnp.int32)
    piece, half, other = spot // 2 % 8, spot % 2, spot // 16
    flip = sum(jnp.where(piece == k, f, 0) for k, (f, _) in enumerate(STEPS))
    step = sum(jnp.where(piece == k, s, 0) for k, (_, s) in enumerate(STEPS))
    xl, y, c = lax.axis_index("xl"), lax.axis_index("y"), lax.axis_index("c")
    return ((((xl + flip) & 1) * 4 + ((y + step) & 3)) * 2 + (c ^ other)) * 2 + half


def return_rows(grad_block, dp_count):
    depth, columns = grad_block.shape
    peak = jnp.max(jnp.abs(grad_block))
    power = jnp.clip(jnp.floor(14.0 - jnp.log2(peak)), -120.0, 120.0)
    scaled = (grad_block * jnp.exp2(power)).reshape(dp_count, depth // dp_count, columns)
    tag = jnp.full((dp_count, 8, columns), power)
    packet = jnp.concatenate([scaled, tag], axis=1).astype(jnp.float16)
    packet = lax.all_to_all(packet, DP, 0, 0, tiled=True).astype(jnp.float32)
    packet = with_layout_constraint(packet, Layout((0, 1, 2)))
    rows = packet[:, :-8] * jnp.exp2(-packet[:, -1:, :1])
    bands = rows.reshape(dp_count, -1, 8, columns).transpose(1, 0, 2, 3)
    bands = lax.optimization_barrier(with_layout_constraint(bands, Layout((0, 1, 2, 3))))
    return bands.transpose(0, 2, 1, 3).reshape(depth // dp_count, dp_count * columns)


def local(passage_hidden, passage_lengths, query_ids, query_lengths, positives, head, df_prev):
    dp_count = lax.axis_size(DP)
    dp_index = lax.axis_index(DP)
    vocab_index = lax.axis_index(VOCAB)
    width_local = head.shape[1]
    column_count = width_local // dp_count
    query_slots = query_ids.shape[1]
    packed = jnp.concatenate([query_ids, query_lengths[:, None], passage_lengths[:, None]], axis=1)
    packed = spread(packed, DP).reshape(-1, query_slots + 2)
    query_tokens = packed[:, :query_slots]
    query_sizes = packed[:, query_slots]
    hidden_all = gather_hidden(passage_hidden)
    passages = gathered_passages()
    passage_count = packed.shape[0]
    placed = passages[:, None] == jnp.arange(passage_count, dtype=jnp.int32)[None, :]
    passage_sizes = jnp.sum(jnp.where(placed, packed[:, query_slots + 1][None, :], 0), axis=1)
    placed = placed.astype(jnp.float32)
    head_block = lax.all_to_all(head, DP, split_axis=1, concat_axis=0, tiled=True)
    seq_span = hidden_all.shape[0] // passage_count
    logits = jnp.dot(hidden_all, head_block, preferred_element_type=jnp.float32)
    softened = jax.nn.softplus(logits)
    activation = jnp.log1p(softened)
    slope_term = jax.nn.sigmoid(logits) / (1.0 + softened)
    positions = jnp.arange(seq_span, dtype=jnp.int32)
    token_mask = (positions[None, :] < passage_sizes[:, None]).astype(jnp.float32)
    token_weight = token_mask / passage_sizes.astype(jnp.float32)[:, None]
    passage_rep = jnp.sum(
        activation.reshape(passage_count, seq_span, column_count) * token_weight[:, :, None], axis=1
    )
    first_column = dp_index * column_count
    doc_freq = lax.dynamic_slice_in_dim(df_prev, first_column, column_count, 0) + jnp.sum(
        1.0 - jnp.exp(-2.0 * passage_rep), axis=0
    )
    term_weight = jnp.log1p(doc_freq)
    column_ids = (
        vocab_index * width_local + first_column + jnp.arange(column_count, dtype=jnp.int32)
    )
    query_mask = jnp.arange(query_slots, dtype=jnp.int32)[None, :] < query_sizes[:, None]
    matches = (query_tokens[:, :, None] == column_ids[None, None, :]) & query_mask[:, :, None]
    query_bag = jnp.sum(matches.astype(jnp.float32), axis=1)
    partial_scores = jnp.dot(
        query_bag,
        passage_rep.T,
        precision=lax.Precision.HIGHEST,
        preferred_element_type=jnp.float32,
    )
    partial_scores = jnp.dot(partial_scores, placed, precision=lax.Precision.HIGHEST)
    query_total = positives.shape[0]
    plane_scores = jnp.sum(spread(partial_scores, PLANE), axis=0)
    scores = jnp.sum(spread(plane_scores, "z"), axis=0)
    score_grad = ranking_grad(scores, positives, query_total)
    score_grad = jnp.dot(placed, score_grad.T, precision=lax.Precision.HIGHEST)
    rep_grad = jnp.dot(
        score_grad, query_bag, precision=lax.Precision.HIGHEST, preferred_element_type=jnp.float32
    )
    rep_grad = rep_grad + 2.0 * flops_weight / passage_count * term_weight * jnp.mean(
        passage_rep, axis=0
    )
    logit_grad = (
        (token_weight[:, :, None] * rep_grad[:, None, :]).reshape(logits.shape) * slope_term
    ).astype(jnp.bfloat16)
    grad_block = lax.dot_general(
        hidden_all, logit_grad, (((0,), (0,)), ((), ())), preferred_element_type=jnp.float32
    )
    return (return_rows(grad_block, dp_count), scores)


def solution(mesh):
    fine = Mesh(mesh.devices.reshape(2, 4, 2, 16, 2), DP + VOCAB)
    return jax.shard_map(
        local,
        mesh=fine,
        in_specs=(
            P(DP, None),
            P(DP),
            P(DP, None),
            P(DP),
            P(),
            P(DP, VOCAB),
            P(VOCAB),
        ),
        out_specs=(P(DP, VOCAB), P()),
        check_vma=False,
    )
```
